32 devices in a mesh: vx: 4 (over y, x), vy: 8 (over z, core).
Axes of the slice: x: 2, y: 2, z: 4, core: 2. Of those that a mesh axis runs over, the one named last changes fastest.
Arguments:
- hidden: bfloat16 [128, 5120], P(('vx', 'vy')), may hold values from -96 to 96
- unembed: bfloat16 [152064, 5120], P(('vx', 'vy')), may hold values from -2 to 2
- loss_mask: int32 [128], P(('vx', 'vy')), may hold values 0 or 1
- seq_ids: int32 [128], P(('vx', 'vy')), may hold values from 0 to 7, never falling along the last dimension, each value on 1 to 32 neighbouring positions
Outputs:
- entropy: float32 [128], P(('vx', 'vy'))
- seq_mean: float32 [8], replicated
The draws below stay inside these ranges and needn't reach their ends.
Inputs may be any that keep to these rules, and one draw needn't show every extreme that they name: `seq_ids`: sequence numbers never fall along the tokens; each sequence has 1 to 32 tokens.
All inputs are finite; a program needn't handle non-finite values. No bound on the sum of `loss_mask` on one device may be relied on, other than what follows from the above.
Results may differ from the reference program's by a relative error of at most 0.0013.
Values may be sent and summed in bfloat16 or wider, within the bound.
A program may use at most 128 MiB of HBM per device.

```python
import math
import jax
import jax.numpy as jnp
import numpy as np
from jax import lax

D = 5120
VOCAB = 152064
SEQS = 8
TOKENS = 128
SEG_MOST = 32
N_VX = 4
N_VY = 8


def unembed_rows(key, indices):

    def single(index):
        base = jax.random.normal(jax.random.fold_in(jax.random.fold_in(key, 11), index), (D,), jnp.float32) * D ** (-0.5)
        return base
    return jax.vmap(single)(indices)


def draw_unembed(key, part):
    rows = unembed_rows(key, jnp.arange(VOCAB, dtype=jnp.int32))
    return jnp.clip(rows, -2.0, 2.0).astype(jnp.bfloat16)


def draw_hidden(key, part):
    base = jax.random.normal(jax.random.fold_in(key, 21), (TOKENS, D), jnp.float32) * 4.0
    return jnp.clip(base, -96.0, 96.0).astype(jnp.bfloat16)


def place_ends(entries, key, smallest, largest):
    longest = entries.shape.index(max(entries.shape))
    spots = []
    for shift in (0, 1):
        where = [jax.random.randint(jax.random.fold_in(key, axis), (), 0, length) for axis, length in enumerate(entries.shape)]
        where[longest] = (where[longest] + shift) % entries.shape[longest]
        spots.append(tuple(where))
    return entries.at[spots[0]].set(smallest).at[spots[1]].set(largest)


def length_profile(count, total, limit, skew):
    weights = [(1 << 20) // math.isqrt(grade ** skew) + 1 for grade in range(2, count + 1)]
    rest, holding = total - limit - (count - 1), [1] * (count - 1)
    while rest > 0:
        free = [i for i in range(count - 1) if holding[i] < limit]
        whole, left = sum([weights[i] for i in free]), rest
        for i in free:
            addition = min(limit - holding[i], max(1, left * weights[i] // whole), rest)
            holding[i] = holding[i] + addition
            rest = rest - addition
    return np.array([limit] + holding)


def uneven(rng, amount, total, limit, slope):
    if amount == 2:
        one = jax.random.randint(rng, (), max(1, total - limit), min(limit, total - 1) + 1)
        return jnp.stack([one, total - one])
    lengths = jnp.asarray(length_profile(amount, total, limit, slope), jnp.int32)
    twos = (amount - 1) // 2
    donor, sink = lengths[1:1 + 2 * twos:2], lengths[2:2 + 2 * twos:2]
    margin = jnp.minimum(donor - 1, limit - sink)
    moved = jax.random.randint(jax.random.fold_in(rng, 1), (twos,), 0, 1 << 20) % (margin + 1)
    lengths = lengths.at[1:1 + 2 * twos:2].set(donor - moved).at[2:2 + 2 * twos:2].set(sink + moved)
    return lengths[jax.random.permutation(jax.random.fold_in(rng, 2), amount)]


def setup_inputs(seed: int = 0) -> dict:
    key_of = jax.random.split(jax.random.key(seed), 5)
    hidden = draw_hidden(jax.random.fold_in(key_of[4], 71), 0)
    unembed = draw_unembed(jax.random.fold_in(key_of[4], 71), 0)
    loss_mask = place_ends((jax.random.randint(key_of[2], (TOKENS,), 0, 4) < 3).astype(jnp.int32), jax.random.fold_in(key_of[2], 1), 0, 1)
    seq_ids = jnp.searchsorted(jnp.cumsum(uneven(key_of[3], SEQS, TOKENS, SEG_MOST, 1)), jnp.arange(TOKENS), side="right").astype(jnp.int32)
    return {"hidden": hidden, "unembed": unembed, "loss_mask": loss_mask, "seq_ids": seq_ids}


def combine_stats(earlier, later):
    joined = jnp.maximum(earlier[0], later[0])
    shift_a = earlier[0] - joined
    shift_b = later[0] - joined
    scale_a = jnp.exp(shift_a)
    scale_b = jnp.exp(shift_b)
    norms = scale_a * earlier[1] + scale_b * later[1]
    tilts = scale_a * (earlier[2] + shift_a * earlier[1]) + scale_b * (later[2] + shift_b * later[1])
    return (joined, norms, tilts)


def block_stats(hidden, block):
    logits = jnp.dot(hidden, block.T, preferred_element_type=jnp.float32)
    peaked = jnp.max(logits, axis=1)
    shifted = logits - peaked[:, None]
    expval = jnp.exp(shifted)
    return (peaked, jnp.sum(expval, axis=1), jnp.sum(expval * shifted, axis=1))


def reference(hidden, unembed, loss_mask, seq_ids):
    pieces = N_VX * N_VY
    span_size = VOCAB // pieces
    blocks = unembed.reshape(pieces, span_size, D)
    initial = block_stats(hidden, blocks[0])

    def advance(carry, block):
        return combine_stats(carry, block_stats(hidden, block)), None

    merged, unused = lax.scan(advance, initial, blocks[1:])
    entropy = jnp.log(merged[1]) - merged[2] / merged[1]
    member = (seq_ids[:, None] == jnp.arange(SEQS, dtype=jnp.int32)[None, :]) & (loss_mask[:, None] > 0)
    seq_sums = jnp.sum(entropy[:, None] * member.astype(jnp.float32), axis=0)
    seq_counts = jnp.sum(member.astype(jnp.int32), axis=0)
    seq_mean = seq_sums / jnp.maximum(seq_counts, 1).astype(jnp.float32)
    return entropy, seq_mean
```

```python
import functools

import jax
import jax.numpy as jnp
from jax import lax
from jax.experimental import pallas as pl
from jax.experimental.pallas import tpu as pltpu
from jax.sharding import PartitionSpec as P

SEQS = 8
CORES = 2
MESH = pl.DeviceIdType.MESH
F32 = jnp.float32


def rows_per_chunk(rows, most=512):
    fits = [c for c in range(16, most + 1, 16) if rows % c == 0]
    return max(fits) if fits else rows


def kernel(
    nx, ny, chunk,
    hidden, unembed, mask, ids,
    entropy, seq_mean,
    weights, blocks, tokens_t, stats, stats_all,
    w_sem, send_sem, recv_sem, own_sem, stat_send, stat_recv,
):
    n, nz = nx * ny, ny // CORES
    tok, depth = hidden.shape
    total = n * tok
    chunks = unembed.shape[0] // chunk
    vx, vy = lax.axis_index("vx"), lax.axis_index("vy")
    z, core = vy // CORES, vy % CORES
    me = vx * ny + vy

    def w_copy(i):
        rows = pl.ds(i * chunk, chunk)
        return pltpu.make_async_copy(unembed.at[rows], weights.at[rows], w_sem.at[i])

    own = pltpu.make_async_copy(hidden, blocks.at[me], own_sem)
    own.start()
    for i in range(chunks):
        w_copy(i).start()

    barrier = pltpu.get_barrier_semaphore()
    for d in range(1, nx):
        pl.semaphore_signal(barrier, inc=1, device_id=((vx + d) % nx, vy), device_id_type=MESH)
    for d in range(1, nz):
        pl.semaphore_signal(
            barrier, inc=1, device_id=(vx, ((z + d) % nz) * CORES + core), device_id_type=MESH
        )
    pl.semaphore_signal(barrier, inc=1, device_id=(vx, z * CORES + 1 - core), device_id_type=MESH)
    pl.semaphore_wait(barrier, nx + nz - 1)

    def send(source, slot, x, y):
        pltpu.make_async_remote_copy(
            src_ref=source, dst_ref=blocks.at[slot], send_sem=send_sem,
            recv_sem=recv_sem.at[slot], device_id=(x, y), device_id_type=MESH,
        ).start()

    def arrived(slot):
        pltpu.make_async_remote_copy(
            src_ref=blocks.at[slot], dst_ref=blocks.at[slot], send_sem=send_sem,
            recv_sem=recv_sem.at[slot], device_id=(vx, vy), device_id_type=MESH,
        ).wait_recv()

    far = sorted(range(1, nz), key=lambda d: min(d, nz - d))

    def along_z(source, slot):
        for d in far:
            send(source, slot, vx, ((z + d) % nz) * CORES + core)

    def to_partner(source, slot):
        send(source, slot, vx, z * CORES + 1 - core)

    for d in range(1, nx):
        send(hidden, me, (vx + d) % nx, vy)
    along_z(hidden, me)
    to_partner(hidden, me)
    for d in range(1, nx):
        slot = ((vx + d) % nx) * ny + vy
        arrived(slot)
        along_z(blocks.at[slot], slot)
        to_partner(blocks.at[slot], slot)
    for e in range(nx):
        for d in far:
            slot = ((vx + e) % nx) * ny + ((z + d) % nz) * CORES + core
            arrived(slot)
            to_partner(blocks.at[slot], slot)
    for e in range(nx):
        for d in range(nz):
            arrived(((vx + e) % nx) * ny + ((z + d) % nz) * CORES + 1 - core)
    own.wait()

    width = 512 if depth % 512 == 0 else depth

    @pl.loop(0, depth // width)
    def _(i):
        cols = pl.ds(pl.multiple_of(i * width, width), width)
        tokens_t[cols, :] = blocks[:, :, cols].reshape(total, width).T

    def step(i, carry):
        peak, norm, tilt = carry
        rows = pl.ds(pl.multiple_of(i * chunk, chunk), chunk)
        w_copy(i).wait()
        logits = jnp.dot(weights[rows, :], tokens_t[...], preferred_element_type=F32)
        top = jnp.maximum(peak, jnp.max(logits, axis=0, keepdims=True))
        shifted = logits - top
        value = jnp.exp(shifted)
        shift = peak - top
        factor = jnp.exp(shift)
        return (
            top,
            factor * norm + jnp.sum(value, axis=0, keepdims=True),
            factor * (tilt + shift * norm) + jnp.sum(value * shifted, axis=0, keepdims=True),
        )

    low = jnp.full((1, total), jnp.finfo(jnp.float32).min / 4, F32)
    zero = jnp.zeros((1, total), F32)
    peak, norm, tilt = lax.fori_loop(0, chunks, step, (low, zero, zero))

    lane = lax.broadcasted_iota(jnp.int32, (1, total), 1)
    code = jnp.zeros((1, total), jnp.int32)
    for j in range(tok):
        mine = jnp.where(mask[j] > 0, ids[j] + 1, 0)
        code = jnp.where(lane == me * tok + j, mine, code)
    stats[0:1, :] = peak
    stats[1:2, :] = norm
    stats[2:3, :] = tilt
    stats[3:4, :] = code.astype(F32)

    def stat_copy(d):
        peer = (me + d) % n
        return pltpu.make_async_remote_copy(
            src_ref=stats, dst_ref=stats_all.at[me], send_sem=stat_send, recv_sem=stat_recv,
            device_id=(peer // ny, peer % ny), device_id_type=MESH,
        )

    @pl.loop(1, n)
    def _(d):
        stat_copy(d).start()

    stats_all[me] = stats[...]
    everyone = pltpu.make_async_remote_copy(
        src_ref=stats_all.at[pl.ds(0, n - 1)], dst_ref=stats_all.at[pl.ds(0, n - 1)],
        send_sem=stat_send, recv_sem=stat_recv, device_id=(vx, vy), device_id_type=MESH,
    )
    everyone.wait_recv()

    peaks, norms, tilts = stats_all[:, 0, :], stats_all[:, 1, :], stats_all[:, 2, :]
    codes = jnp.sum(stats_all[:, 3, :], axis=0, keepdims=True)
    shift = peaks - jnp.max(peaks, axis=0, keepdims=True)
    factor = jnp.exp(shift)
    norm = jnp.sum(factor * norms, axis=0, keepdims=True)
    tilt = jnp.sum(factor * (tilts + shift * norms), axis=0, keepdims=True)
    value = jnp.log(norm) - tilt / norm

    slot = lax.broadcasted_iota(jnp.int32, (1, tok), 1)
    out = jnp.zeros((1, tok), F32)
    for j in range(tok):
        one = jnp.sum(jnp.where(lane == me * tok + j, value, 0.0), axis=1, keepdims=True)
        out = jnp.where(slot == j, one, out)
    entropy[...] = out
    seq = lax.broadcasted_iota(jnp.int32, (SEQS, total), 0)
    member = (jnp.broadcast_to(codes, (SEQS, total)) == (seq + 1).astype(F32)).astype(F32)
    sums = jnp.sum(member * jnp.broadcast_to(value, (SEQS, total)), axis=1, keepdims=True)
    counts = jnp.sum(member, axis=1, keepdims=True)
    mean = sums / jnp.maximum(counts, 1.0)
    diag = lax.broadcasted_iota(jnp.int32, (SEQS, SEQS), 0) == lax.broadcasted_iota(
        jnp.int32, (SEQS, SEQS), 1
    )
    seq_mean[...] = jnp.sum(jnp.where(diag, mean, 0.0), axis=0, keepdims=True)

    everyone.wait_send()
    pltpu.make_async_remote_copy(
        src_ref=blocks.at[pl.ds(0, n - 1)], dst_ref=blocks.at[pl.ds(0, n - 1)],
        send_sem=send_sem, recv_sem=own_sem, device_id=(vx, vy), device_id_type=MESH,
    ).wait_send()


def solution(mesh):
    nx, ny = mesh.shape["vx"], mesh.shape["vy"]
    n = nx * ny

    def per_device(hidden, unembed, loss_mask, seq_ids):
        tok, depth = hidden.shape
        rows, total = unembed.shape[0], tok * n
        chunk = rows_per_chunk(rows)
        entropy, seq_mean = pl.pallas_call(
            functools.partial(kernel, nx, ny, chunk),
            out_shape=[
                jax.ShapeDtypeStruct((1, tok), F32),
                jax.ShapeDtypeStruct((1, SEQS), F32),
            ],
            in_specs=[pl.BlockSpec(memory_space=pl.ANY)] * 2
            + [pl.BlockSpec(memory_space=pltpu.SMEM)] * 2,
            out_specs=[pl.BlockSpec(memory_space=pltpu.VMEM)] * 2,
            scratch_shapes=[
                pltpu.VMEM((rows, depth), jnp.bfloat16),
                pltpu.VMEM((n, tok, depth), jnp.bfloat16),
                pltpu.VMEM((depth, total), jnp.bfloat16),
                pltpu.VMEM((8, total), F32),
                pltpu.VMEM((n, 8, total), F32),
                pltpu.SemaphoreType.DMA((rows // chunk,)),
                pltpu.SemaphoreType.DMA,
                pltpu.SemaphoreType.DMA((n,)),
                pltpu.SemaphoreType.DMA,
                pltpu.SemaphoreType.DMA,
                pltpu.SemaphoreType.DMA,
            ],
            compiler_params=pltpu.CompilerParams(
                collective_id=0, has_side_effects=True, vmem_limit_bytes=62 * 1024 * 1024
            ),
        )(hidden, unembed, loss_mask, seq_ids)
        return entropy.reshape(tok), seq_mean.reshape(SEQS)

    in_specs = (P(("vx", "vy"), None), P(("vx", "vy"), None), P(("vx", "vy")), P(("vx", "vy")))
    return jax.shard_map(
        per_device, mesh=mesh, in_specs=in_specs, out_specs=(P(("vx", "vy")), P()), check_vma=False
    )
```

```python
import functools

import jax
import jax.numpy as jnp
from jax import lax
from jax.experimental import pallas as pl
from jax.experimental.pallas import tpu as pltpu
from jax.sharding import PartitionSpec as P

SEQS = 8
CORES = 2
MESH = pl.DeviceIdType.MESH
F32 = jnp.float32


def rows_per_chunk(rows, most=512):
    fits = [c for c in range(16, most + 1, 16) if rows % c == 0]
    return max(fits) if fits else rows


def kernel(
    nx, ny, chunk,
    hidden, unembed, mask, ids,
    entropy, seq_mean,
    weights, blocks, tokens_t, stats, stats_all,
    w_sem, send_sem, recv_sem, own_sem, stat_send, stat_recv,
):
    n, nz = nx * ny, ny // CORES
    tok, depth = hidden.shape
    total = n * tok
    chunks = unembed.shape[0] // chunk
    vx, vy = lax.axis_index("vx"), lax.axis_index("vy")
    z, core = vy // CORES, vy % CORES
    me = vx * ny + vy

    def w_copy(i):
        rows = pl.ds(i * chunk, chunk)
        return pltpu.make_async_copy(unembed.at[rows], weights.at[rows], w_sem.at[i])

    own = pltpu.make_async_copy(hidden, blocks.at[me], own_sem)
    own.start()
    for i in range(chunks):
        w_copy(i).start()

    barrier = pltpu.get_barrier_semaphore()
    for d in range(1, nx):
        pl.semaphore_signal(barrier, inc=1, device_id=((vx + d) % nx, vy), device_id_type=MESH)
    for d in range(1, nz):
        pl.semaphore_signal(
            barrier, inc=1, device_id=(vx, ((z + d) % nz) * CORES + core), device_id_type=MESH
        )
    pl.semaphore_signal(barrier, inc=1, device_id=(vx, z * CORES + 1 - core), device_id_type=MESH)
    pl.semaphore_wait(barrier, nx + nz - 1)

    def send(source, slot, x, y):
        pltpu.make_async_remote_copy(
            src_ref=source, dst_ref=blocks.at[slot], send_sem=send_sem,
            recv_sem=recv_sem.at[slot], device_id=(x, y), device_id_type=MESH,
        ).start()

    def arrived(slot):
        pltpu.make_async_remote_copy(
            src_ref=blocks.at[slot], dst_ref=blocks.at[slot], send_sem=send_sem,
            recv_sem=recv_sem.at[slot], device_id=(vx, vy), device_id_type=MESH,
        ).wait_recv()

    far = sorted(range(1, nz), key=lambda d: min(d, nz - d))

    def along_z(source, slot):
        for d in far:
            send(source, slot, vx, ((z + d) % nz) * CORES + core)

    def to_partner(source, slot):
        send(source, slot, vx, z * CORES + 1 - core)

    along_z(hidden, me)
    for d in range(1, nx):
        send(hidden, me, (vx + d) % nx, vy)
    to_partner(hidden, me)
    for e in far:
        slot = vx * ny + ((z + e) % nz) * CORES + core
        arrived(slot)
        for d in range(1, nx):
            send(blocks.at[slot], slot, (vx + d) % nx, vy)
        to_partner(blocks.at[slot], slot)
    for e in [0] + far:
        for d in range(1, nx):
            slot = ((vx + d) % nx) * ny + ((z + e) % nz) * CORES + core
            arrived(slot)
            to_partner(blocks.at[slot], slot)
    for e in range(nx):
        for d in range(nz):
            arrived(((vx + e) % nx) * ny + ((z + d) % nz) * CORES + 1 - core)
    own.wait()

    width = 512 if depth % 512 == 0 else depth

    @pl.loop(0, depth // width)
    def _(i):
        cols = pl.ds(pl.multiple_of(i * width, width), width)
        tokens_t[cols, :] = blocks[:, :, cols].reshape(total, width).T

    def step(i, carry):
        peak, norm, tilt = carry
        rows = pl.ds(pl.multiple_of(i * chunk, chunk), chunk)
        w_copy(i).wait()
        logits = jnp.dot(weights[rows, :], tokens_t[...], preferred_element_type=F32)
        top = jnp.maximum(peak, jnp.max(logits, axis=0, keepdims=True))
        shifted = logits - top
        value = jnp.exp(shifted)
        shift = peak - top
        factor = jnp.exp(shift)
        return (
            top,
            factor * norm + jnp.sum(value, axis=0, keepdims=True),
            factor * (tilt + shift * norm) + jnp.sum(value * shifted, axis=0, keepdims=True),
        )

    low = jnp.full((1, total), jnp.finfo(jnp.float32).min / 4, F32)
    zero = jnp.zeros((1, total), F32)
    peak, norm, tilt = lax.fori_loop(0, chunks, step, (low, zero, zero))

    lane = lax.broadcasted_iota(jnp.int32, (1, total), 1)
    code = jnp.zeros((1, total), jnp.int32)
    for j in range(tok):
        mine = jnp.where(mask[j] > 0, ids[j] + 1, 0)
        code = jnp.where(lane == me * tok + j, mine, code)
    stats[0:1, :] = peak
    stats[1:2, :] = norm
    stats[2:3, :] = tilt
    stats[3:4, :] = code.astype(F32)

    def stat_copy(d):
        peer = (me + d) % n
        return pltpu.make_async_remote_copy(
            src_ref=stats, dst_ref=stats_all.at[me], send_sem=stat_send, recv_sem=stat_recv,
            device_id=(peer // ny, peer % ny), device_id_type=MESH,
        )

    @pl.loop(1, n)
    def _(d):
        stat_copy(d).start()

    stats_all[me] = stats[...]
    everyone = pltpu.make_async_remote_copy(
        src_ref=stats_all.at[pl.ds(0, n - 1)], dst_ref=stats_all.at[pl.ds(0, n - 1)],
        send_sem=stat_send, recv_sem=stat_recv, device_id=(vx, vy), device_id_type=MESH,
    )
    everyone.wait_recv()

    peaks, norms, tilts = stats_all[:, 0, :], stats_all[:, 1, :], stats_all[:, 2, :]
    codes = jnp.sum(stats_all[:, 3, :], axis=0, keepdims=True)
    shift = peaks - jnp.max(peaks, axis=0, keepdims=True)
    factor = jnp.exp(shift)
    norm = jnp.sum(factor * norms, axis=0, keepdims=True)
    tilt = jnp.sum(factor * (tilts + shift * norms), axis=0, keepdims=True)
    value = jnp.log(norm) - tilt / norm

    slot = lax.broadcasted_iota(jnp.int32, (1, tok), 1)
    out = jnp.zeros((1, tok), F32)
    for j in range(tok):
        one = jnp.sum(jnp.where(lane == me * tok + j, value, 0.0), axis=1, keepdims=True)
        out = jnp.where(slot == j, one, out)
    entropy[...] = out
    seq = lax.broadcasted_iota(jnp.int32, (SEQS, total), 0)
    member = (jnp.broadcast_to(codes, (SEQS, total)) == (seq + 1).astype(F32)).astype(F32)
    sums = jnp.sum(member * jnp.broadcast_to(value, (SEQS, total)), axis=1, keepdims=True)
    counts = jnp.sum(member, axis=1, keepdims=True)
    mean = sums / jnp.maximum(counts, 1.0)
    diag = lax.broadcasted_iota(jnp.int32, (SEQS, SEQS), 0) == lax.broadcasted_iota(
        jnp.int32, (SEQS, SEQS), 1
    )
    seq_mean[...] = jnp.sum(jnp.where(diag, mean, 0.0), axis=0, keepdims=True)

    everyone.wait_send()
    pltpu.make_async_remote_copy(
        src_ref=blocks.at[pl.ds(0, n - 1)], dst_ref=blocks.at[pl.ds(0, n - 1)],
        send_sem=send_sem, recv_sem=own_sem, device_id=(vx, vy), device_id_type=MESH,
    ).wait_send()


def solution(mesh):
    nx, ny = mesh.shape["vx"], mesh.shape["vy"]
    n = nx * ny

    def per_device(hidden, unembed, loss_mask, seq_ids):
        tok, depth = hidden.shape
        rows, total = unembed.shape[0], tok * n
        chunk = rows_per_chunk(rows)
        entropy, seq_mean = pl.pallas_call(
            functools.partial(kernel, nx, ny, chunk),
            out_shape=[
                jax.ShapeDtypeStruct((1, tok), F32),
                jax.ShapeDtypeStruct((1, SEQS), F32),
            ],
            in_specs=[pl.BlockSpec(memory_space=pltpu.VMEM), pl.BlockSpec(memory_space=pl.ANY)]
            + [pl.BlockSpec(memory_space=pltpu.SMEM)] * 2,
            out_specs=[pl.BlockSpec(memory_space=pltpu.VMEM)] * 2,
            scratch_shapes=[
                pltpu.VMEM((rows, depth), jnp.bfloat16),
                pltpu.VMEM((n, tok, depth), jnp.bfloat16),
                pltpu.VMEM((depth, total), jnp.bfloat16),
                pltpu.VMEM((4, total), F32),
                pltpu.VMEM((n, 4, total), F32),
                pltpu.SemaphoreType.DMA((rows // chunk,)),
                pltpu.SemaphoreType.DMA,
                pltpu.SemaphoreType.DMA((n,)),
                pltpu.SemaphoreType.DMA,
                pltpu.SemaphoreType.DMA,
                pltpu.SemaphoreType.DMA,
            ],
            compiler_params=pltpu.CompilerParams(
                collective_id=0, has_side_effects=True, vmem_limit_bytes=62 * 1024 * 1024
            ),
        )(hidden, unembed, loss_mask, seq_ids)
        return entropy.reshape(tok), seq_mean.reshape(SEQS)

    in_specs = (P(("vx", "vy"), None), P(("vx", "vy"), None), P(("vx", "vy")), P(("vx", "vy")))
    return jax.shard_map(
        per_device, mesh=mesh, in_specs=in_specs, out_specs=(P(("vx", "vy")), P()), check_vma=False
    )
```
